256 devices in a mesh: pole: 8 (over y, x_lo), leaf: 32 (over x_hi, z, core).
Axes of the slice: x: 4 (x_hi: 2, x_lo: 2; x = x_hi * 2 + x_lo), y: 4, z: 8, core: 2. Of those that a mesh axis runs over, the one named last changes fastest.
Arguments:
- inverse_front: bfloat16 [8, 2, 8192, 8192], P('pole', None, 'leaf'), may hold values from -6 to 6
- factor_panel: bfloat16 [8, 8192, 512], P('pole', 'leaf'), may hold values from -0.0625 to 0.0625
- diag_inverse: bfloat16 [8, 256, 512], P('pole'), may hold values from -6 to 6
- pole_weight: float32 [8, 2], P('pole'), may hold values from -2.4 to 2.4
- structure: int32 [32], replicated, may hold values from 0 to 1, as said below
- block_owner: int32 [1024, 1], P('leaf'), may hold values from 0 to 31; in each aligned block of 32 rows (0 to 31, 32 to 63, ...) at most 2 rows name the same one
Outputs:
- owned_density: float32 [2048, 8, 256], P('leaf')
- diag_density: float32 [256, 256], replicated
The draws below stay inside these ranges and needn't reach their ends.
Inputs may be any that keep to these rules, and one draw needn't show every extreme that they name: `structure`: exactly 16 entries are 1. `block_owner`: among the 32 blocks of one index of leaf no owner appears more than 2 times, and in some index's blocks one owner appears exactly 2 times.
All inputs are finite; a program needn't handle non-finite values.
Results may differ from the reference program's by a relative error of at most 0.0003.
Values may be sent and summed in bfloat16 or wider, within the bound.
No kernel may reach another device: no remote copies, remote signals or barrier semaphores. Data moves between devices by JAX's collectives and lax.ppermute only.
A program may use at most 64 MiB of HBM per device.

```python
import math
import jax
import jax.numpy as jnp
import numpy as np
from jax import lax

SN = 256
NF = 8192
RB = 8
POLES = 8
NBR = 32
NSEL = 16
NB = 1024
NB_DEV = 32
CAP = 2
SLOTS = 64
TOTAL_SLOTS = 2048
N_LEAF = 32


def draw_structure(key, part):
    order = jax.random.permutation(key, NBR).astype(jnp.int32)
    return (order < NSEL).astype(jnp.int32)


def level_of(rng, extent, pieces, smallest, high):
    loudness, own = 1.0, jax.random.fold_in(rng, 6)
    for axis_at, parts in pieces:
        steps = jnp.exp(jax.random.uniform(jax.random.fold_in(own, axis_at), (parts,), jnp.float32, smallest / len(pieces), high / len(pieces)))
        loudness = loudness * jnp.repeat(steps, extent[axis_at] // parts).reshape([-1 if axis == axis_at else 1 for axis in range(len(extent))])
    return loudness


def routed_block(rng, own, number, rows, number_of, top, reach, slope):
    ranking = jax.random.permutation(rng, number_of)
    heavy_load, usual = load_shares(number_of, rows * top, reach, slope, True), load_shares(number_of, rows * top, reach, slope, False)
    places = jnp.arange(number_of)

    def named(lengths, offset_by):
        used = int((lengths > 0).sum())
        fixed = max(1, used // 4)
        moved = fixed + (places - fixed + offset_by * (used - fixed)) % max(1, number_of - fixed)
        return jnp.zeros((number_of,), jnp.int32).at[ranking[jnp.where(places < fixed, places, moved)]].set(jnp.asarray(lengths, jnp.int32))

    lengths = jnp.where(number % 4 == 0, named(heavy_load, number // 4), named(usual, number - number // 4 - 1))
    mixed = jax.random.permutation(jax.random.fold_in(own, 3), number_of)
    source_of, taker = mixed[0:number_of // 2 * 2:2], mixed[1:number_of // 2 * 2:2]
    slack = jnp.minimum(lengths[source_of] - 1, reach - lengths[taker]) // 2
    slack = jnp.where((source_of == ranking[0]) | (taker == ranking[0]) | (lengths[taker] == 0), 0, jnp.maximum(slack, 0))
    moved = jax.random.randint(jax.random.fold_in(own, 4), (number_of // 2,), 0, 1 << 20) % (slack + 1)
    lengths = lengths.at[source_of].add(-moved).at[taker].add(moved)
    labels = jnp.searchsorted(jnp.cumsum(lengths), jnp.arange(rows * top), side="right").astype(jnp.int32)
    table = labels.reshape(top, rows).T
    table = table[jax.random.permutation(jax.random.fold_in(own, 1), rows)]
    offset_by = jax.random.randint(jax.random.fold_in(own, 2), (rows, 1), 0, top)
    return jnp.take_along_axis(table, (jnp.arange(top)[None, :] + offset_by) % top, axis=1)


def load_shares(amount, total, most, lean, full):
    weights = [(1 << 20) // math.isqrt(standing ** lean) + 1 for standing in range(1, amount + 1)]
    largest = most if full else min(most, max(-(-total // amount), total * weights[0] // sum(weights)))
    least = 1 if total - largest >= amount - 1 else 0
    counts, spare = [largest] + [least] * (amount - 1), total - largest - least * (amount - 1)
    while spare > 0:
        free = [i for i in range(1, amount) if counts[i] < largest] or [i for i in range(1, amount) if counts[i] < most]
        mass, budget = sum([weights[i] for i in free]), spare
        for i in free:
            extra = min(most - counts[i], max(1, budget * weights[i] // mass), spare)
            counts[i] = counts[i] + extra
            spare = spare - extra
    return np.array(counts)


def gaussian(stream_key, shape, scale, reach, pieces=(), kind=jnp.bfloat16):
    level = level_of(stream_key, shape, pieces, -0.22, 0.18) if pieces else 1.0
    entries = jax.random.normal(stream_key, shape, jnp.float32) * scale * level
    return jnp.minimum(jnp.maximum(entries, -reach), reach).astype(kind)


def setup_inputs(seed: int = 0) -> dict:
    seeds = jax.random.split(jax.random.key(seed), 7)
    inverse_front = gaussian(seeds[0], (POLES, 2, NF, NF), 1.0, 6.0, ((0, 8), (2, 32)))
    factor_panel = gaussian(seeds[1], (POLES, NF, 2 * SN), NF ** -0.5, 0.0625, ((0, 8), (1, 32)))
    diag_inverse = gaussian(seeds[2], (POLES, SN, 2 * SN), 1.0, 6.0, ((0, 8),))
    pole_weight = gaussian(seeds[3], (POLES, 2), 0.4, 2.4, ((0, 8),), jnp.float32)
    structure = draw_structure(jax.random.fold_in(seeds[6], 71), 0)
    block_owner_keys = jax.random.split(jax.random.fold_in(seeds[5], 1), NB // NB_DEV)
    block_owner_turns = jax.random.permutation(jax.random.fold_in(seeds[5], 3), NB // NB_DEV)
    block_owner = jax.vmap(lambda own, number: routed_block(jax.random.fold_in(seeds[5], 2), own, number, NB_DEV, N_LEAF, 1, CAP, 2))(block_owner_keys, block_owner_turns).reshape((NB, 1))
    return {"inverse_front": inverse_front, "factor_panel": factor_panel, "diag_inverse": diag_inverse, "pole_weight": pole_weight, "structure": structure, "block_owner": block_owner}


def chosen_rows(structure):
    order = jnp.argsort(1 - structure, stable=True)[:NSEL].astype(jnp.int32)
    return (order[:, None] * SN + jnp.arange(SN, dtype=jnp.int32)[None, :]).reshape(-1).astype(jnp.int32)


def reference(inverse_front, factor_panel, diag_inverse, pole_weight, structure, block_owner):
    precise = lax.Precision.HIGHEST
    selected = chosen_rows(structure)
    keep_rows = jnp.repeat(structure, SN).astype(jnp.float32)[:, None]

    def one_pole(carried, inputs):
        front_pole, panel_pole, diag_pole, weight_pole = inputs
        panel_used = jnp.take(panel_pole, selected, axis=0).astype(jnp.float32)
        column_real = jnp.take(front_pole[0], selected, axis=1).astype(jnp.float32)
        column_imag = jnp.take(front_pole[1], selected, axis=1).astype(jnp.float32)
        from_real = jnp.dot(column_real, panel_used, precision=precise)
        from_imag = jnp.dot(column_imag, panel_used, precision=precise)
        block_real = -(from_real[:, :SN] - from_imag[:, SN:]) * keep_rows
        block_imag = -(from_real[:, SN:] + from_imag[:, :SN]) * keep_rows
        panel_kept = panel_pole.astype(jnp.float32) * keep_rows
        panel_real = panel_kept[:, :SN]
        panel_imag = panel_kept[:, SN:]
        schur_real = jnp.dot(panel_real.T, block_real, precision=precise) - jnp.dot(panel_imag.T, block_imag, precision=precise)
        schur_imag = jnp.dot(panel_real.T, block_imag, precision=precise) + jnp.dot(panel_imag.T, block_real, precision=precise)
        diag_full = diag_pole.astype(jnp.float32)
        corner_real = diag_full[:, :SN] - schur_real
        corner_imag = diag_full[:, SN:] - schur_imag
        weight_real = weight_pole[0]
        weight_imag = weight_pole[1]
        density_rows = weight_real * block_imag + weight_imag * block_real
        density_corner = weight_real * corner_imag + weight_imag * corner_real
        return (carried[0] + density_rows, carried[1] + density_corner), None

    start_state = (jnp.zeros((NF, SN), jnp.float32), jnp.zeros((SN, SN), jnp.float32))
    (density, diag_density), _ = lax.scan(one_pole, start_state, (inverse_front, factor_panel, diag_inverse, pole_weight))

    blocks = density.reshape(NB, RB, SN)
    owners = block_owner[:, 0]
    sources = (jnp.arange(NB, dtype=jnp.int32) // NB_DEV).astype(jnp.int32)
    one_hot = (owners[:, None] == jnp.arange(N_LEAF, dtype=jnp.int32)[None, :]).astype(jnp.int32)
    grouped = one_hot.reshape(N_LEAF, NB_DEV, N_LEAF)
    earlier = (jnp.cumsum(grouped, axis=1) - grouped).reshape(NB, N_LEAF)
    ranks = jnp.sum(earlier * one_hot, axis=1).astype(jnp.int32)
    slot_index = (owners * SLOTS + sources * CAP + ranks).astype(jnp.int32)
    owned_density = jnp.zeros((TOTAL_SLOTS, RB, SN), jnp.float32).at[slot_index].set(blocks)
    return owned_density, diag_density
```

```python
import jax
import jax.numpy as jnp
from jax import lax
from jax.experimental import pallas as pl
from jax.experimental.pallas import tpu as pltpu
from jax.sharding import Mesh, PartitionSpec as P

LEAF = ("xh", "z", "c")
GROUP = ("pole", "c")
CHIPS = ("xh", "z")
XH, Z, C, POLES = 2, 8, 2, 8
LEAVES = XH * Z * C
SN = 256
HALF = SN // 2
RB = 8
BLOCKS = 32
SEL = 16
F32 = jnp.float32
BF16 = jnp.bfloat16


def leaf_perm(move):
    pairs = []
    for xh in range(XH):
        for z in range(Z):
            for c in range(C):
                a, b, d = move(xh, z, c)
                pairs.append(((xh * Z + z) * C + c, ((a % XH) * Z + b % Z) * C + d % C))
    return pairs


Z_UP = leaf_perm(lambda xh, z, c: (xh, z + 1, c))
Z_DOWN = leaf_perm(lambda xh, z, c: (xh, z - 1, c))
X_SWAP = leaf_perm(lambda xh, z, c: (xh + 1, z, c))
C_SWAP = leaf_perm(lambda xh, z, c: (xh, z, c + 1))


def send(value, perm):
    return lax.ppermute(value, LEAF, perm)


def vmem():
    return pl.BlockSpec(memory_space=pltpu.VMEM)


def smem():
    return pl.BlockSpec(memory_space=pltpu.SMEM)


def pick_kernel(sel_ref, front_ref, out_ref):
    out_ref[0] = front_ref[0].reshape(2 * SN, SN)


def pick_front(sel, front):
    return pl.pallas_call(
        pick_kernel,
        grid_spec=pltpu.PrefetchScalarGridSpec(
            num_scalar_prefetch=1,
            grid=(SEL,),
            in_specs=[pl.BlockSpec((1, 2, SN, SN), lambda r, sel: (0, 0, 0, sel[r]))],
            out_specs=pl.BlockSpec((1, 2 * SN, SN), lambda r, sel: (r, 0, 0)),
        ),
        out_shape=jax.ShapeDtypeStruct((SEL, 2 * SN, SN), BF16),
        name="pick_front",
    )(sel, front)


def add_products(meta_ref, front_ref, acc_ref, pieces):
    for piece, places in pieces:
        for half, place in enumerate(places):

            @pl.when(meta_ref[place] == 1)
            def _(piece=piece, half=half, place=place):
                acc_ref[...] += jnp.dot(
                    front_ref[meta_ref[LEAVES + place]],
                    piece[half * SN : (half + 1) * SN, :],
                    preferred_element_type=F32,
                )


def partial_product(meta, front, acc, pieces, places):
    given = 0 if acc is None else 1

    def kernel(meta_ref, front_ref, *refs):
        out_ref = refs[-1]
        out_ref[...] = refs[0][...] if given else jnp.zeros_like(out_ref)
        add_products(meta_ref, front_ref, out_ref, list(zip(refs[given:-1], places)))

    return pl.pallas_call(
        kernel,
        in_specs=[smem(), vmem()] + [vmem()] * (given + len(pieces)),
        out_specs=vmem(),
        out_shape=jax.ShapeDtypeStruct((2 * SN, 2 * SN), F32),
        input_output_aliases={2: 0} if given else {},
        name="partial_product",
    )(meta, front, *([acc] if given else []), *pieces)


def three_parts(value):
    first = value.astype(BF16)
    rest = value - first.astype(F32)
    second = rest.astype(BF16)
    return first, second, (rest - second.astype(F32)).astype(BF16)


def last_product(meta, weight, front, acc, panel_t, diag, pieces, places):
    def kernel(meta_ref, weight_ref, front_ref, acc_in, panel_ref, diag_ref, *refs):
        out_ref, acc_ref, den_ref, cor_ref = refs[-4:]
        acc_ref[...] = acc_in[...]
        add_products(meta_ref, front_ref, acc_ref, list(zip(refs[:-4], places)))
        keep = meta_ref[2 * LEAVES].astype(F32)
        lead = meta_ref[2 * LEAVES + 1].astype(F32)
        wr = weight_ref[0, 0]
        wi = weight_ref[0, 1]
        block_real = -(acc_ref[:SN, :SN] - acc_ref[SN:, SN:]) * keep
        block_imag = -(acc_ref[:SN, SN:] + acc_ref[SN:, :SN]) * keep
        density = wr * block_imag + wi * block_real
        other = wr * block_real - wi * block_imag
        den_ref[0] = density[:, :HALF]
        den_ref[1] = density[:, HALF:]
        schur = jnp.zeros((SN, SN), F32)
        for left, parts in ((panel_ref[:SN], three_parts(density)), (panel_ref[SN:], three_parts(other))):
            for part in parts:
                schur += jnp.dot(left, part, preferred_element_type=F32)
        diag_real = diag_ref[0, :, :SN].astype(F32)
        diag_imag = diag_ref[0, :, SN:].astype(F32)
        cor_ref[...] = lead * (wr * diag_imag + wi * diag_real) - schur
        for q in range(POLES):
            for c in range(C):
                g = q * C + c
                out_ref[g, :BLOCKS] = den_ref[c, pl.ds(q, BLOCKS, stride=RB), :]
                out_ref[g, BLOCKS : BLOCKS + 16] = cor_ref[16 * g : 16 * g + 16, :HALF]
                out_ref[g, BLOCKS + 16 :] = cor_ref[16 * g : 16 * g + 16, HALF:]

    return pl.pallas_call(
        kernel,
        in_specs=[smem(), smem()] + [vmem()] * (4 + len(pieces)),
        out_specs=vmem(),
        out_shape=jax.ShapeDtypeStruct((POLES * C, 64, HALF), F32),
        scratch_shapes=[pltpu.VMEM((2 * SN, 2 * SN), F32), pltpu.VMEM((C, SN, HALF), F32), pltpu.VMEM((SN, SN), F32)],
        name="last_product",
    )(meta, weight, front, acc, panel_t, diag, *pieces)


def route_kernel(place_ref, got_ref, out_ref, row_ref):
    corner = got_ref[0, BLOCKS:]
    for g in range(1, POLES * C):
        corner += got_ref[g, BLOCKS:]
    for c in range(C):
        rows = got_ref[c, :BLOCKS]
        for q in range(1, POLES):
            rows += got_ref[q * C + c, :BLOCKS]
        row_ref[c * BLOCKS : (c + 1) * BLOCKS] = rows
    for h in range(XH * Z):
        out_ref[h, :8] = jnp.zeros((8, HALF), F32)
        out_ref[h, 8:] = corner
    for b in range(C * BLOCKS):
        place = place_ref[b]
        out_ref[place // 8, pl.ds(place % 8, 1), :] = row_ref[b : b + 1, :]


def route(place, got):
    return pl.pallas_call(
        route_kernel,
        in_specs=[smem(), vmem()],
        out_specs=vmem(),
        out_shape=jax.ShapeDtypeStruct((XH * Z, 40, HALF), F32),
        scratch_shapes=[pltpu.VMEM((C * BLOCKS, HALF), F32)],
        name="route",
    )(place, got)


def spread_kernel(got_ref, out_ref):
    corner = got_ref[0, 8:]
    for h in range(1, XH * Z):
        corner += got_ref[h, 8:]
    for c in range(C):
        for q in range(POLES):
            g = q * C + c
            for h in range(XH * Z):
                out_ref[g, 4 * h : 4 * h + 4] = got_ref[h, 4 * c : 4 * c + 4]
            out_ref[g, 64:] = corner


def spread(got):
    return pl.pallas_call(
        spread_kernel,
        in_specs=[vmem()],
        out_specs=vmem(),
        out_shape=jax.ShapeDtypeStruct((POLES * C, 96, HALF), F32),
        name="spread",
    )(got)


def finish_kernel(got_ref, owned_ref, diag_ref, row_ref):
    for q in range(POLES):
        for c in range(C):
            g = q * C + c
            row_ref[c, pl.ds(q, 64, stride=RB), :] = got_ref[g, :64]
            diag_ref[16 * g : 16 * g + 16, :HALF] = got_ref[g, 64:80]
            diag_ref[16 * g : 16 * g + 16, HALF:] = got_ref[g, 80:]
    for c in range(C):
        owned_ref[:, c * HALF : (c + 1) * HALF] = row_ref[c]


def finish(got):
    return pl.pallas_call(
        finish_kernel,
        in_specs=[vmem()],
        out_specs=[vmem(), vmem()],
        out_shape=[jax.ShapeDtypeStruct((64 * RB, SN), F32), jax.ShapeDtypeStruct((SN, SN), F32)],
        scratch_shapes=[pltpu.VMEM((C, 64 * RB, HALF), F32)],
        name="finish",
    )(got)


def body(inverse_front, factor_panel, diag_inverse, pole_weight, structure, block_owner):
    xh, z, c = (lax.axis_index(name) for name in LEAF)
    own = factor_panel[0]

    dz = jnp.array([0, 0, -1, -1, 1, 1, -2, -2, 2, 2, -3, -3, 3, 3, 4, 4], jnp.int32)
    dx = jnp.array([0, 1] * 8, jnp.int32)
    chip = ((xh + dx) % XH) * Z + (z + dz) % Z
    origin = jnp.concatenate([chip * C + c, chip * C + (1 - c)])
    ids = jnp.arange(LEAVES, dtype=jnp.int32)
    kept = jnp.sum(jnp.where(origin[:, None] == ids[None, :], structure[None, :], 0), axis=1)
    place = jnp.sum(jnp.where(ids[None, :] < ids[:, None], kept[None, :], 0), axis=1)
    chosen = jnp.sum(
        jnp.where((place[None, :] == ids[:SEL, None]) & (kept[None, :] == 1), origin[None, :], 0), axis=1
    )
    lead = (origin[:1] == 0).astype(jnp.int32)
    meta = jnp.concatenate([kept, jnp.minimum(place, SEL - 1), kept[:1], lead])

    owners = block_owner[:, 0]
    same = (owners[:, None] == owners[None, :]) & (ids[None, :] < ids[:, None])
    slot = owners * 2 + jnp.sum(same.astype(jnp.int32), axis=1)
    slot_other = send(slot, C_SWAP)
    slots = jnp.concatenate([jnp.where(c == 0, slot, slot_other), jnp.where(c == 0, slot_other, slot)])
    source = jnp.arange(C * BLOCKS, dtype=jnp.int32) // BLOCKS
    rows = (slots // 4) * 8 + ((slots // 2) % 2) * 4 + source * 2 + slots % 2

    front = pick_front(chosen, inverse_front)

    pair = jnp.concatenate([own, send(own, X_SWAP)], axis=0)
    up, down = [pair], [pair]
    for _ in range(3):
        up.append(send(up[-1], Z_UP))
        down.append(send(down[-1], Z_DOWN))
    up_last = send(up[3][:SN], Z_UP)
    down_last = send(down[3][SN:], Z_DOWN)
    pieces = [pair, up[1], down[1], up[2], down[2], up[3], down[3], up_last, down_last]
    places = [(0, 1), (2, 3), (4, 5), (6, 7), (8, 9), (10, 11), (12, 13), (14,), (15,)]
    other = [send(piece, C_SWAP) for piece in pieces]
    other_places = [tuple(p + 16 for p in two) for two in places]

    def some(first, last):
        return pieces[first:last] + other[first:last], places[first:last] + other_places[first:last]

    acc = partial_product(meta, front, None, *some(0, 3))
    acc = partial_product(meta, front, acc, *some(3, 5))
    parts = last_product(meta, pole_weight, front, acc, own.T, diag_inverse, *some(5, 9))
    parts = lax.all_to_all(parts, GROUP, 0, 0, tiled=True)
    parts = lax.all_to_all(route(rows, parts), CHIPS, 0, 0, tiled=True)
    parts = lax.all_to_all(spread(parts), GROUP, 0, 0, tiled=True)
    owned, diag = finish(parts)
    return owned.reshape(64, RB, SN), diag


def solution(mesh):
    split = Mesh(mesh.devices.reshape(POLES, XH, Z, C), ("pole", "xh", "z", "c"))
    placed = (
        P("pole", None, LEAF, None),
        P("pole", LEAF, None),
        P("pole", None, None),
        P("pole", None),
        P(),
        P(LEAF, None),
    )
    return jax.shard_map(
        body, mesh=split, in_specs=placed, out_specs=(P(LEAF, None, None), P()), check_vma=False
    )
```

```python
import jax
import jax.numpy as jnp
from jax import lax
from jax.experimental import pallas as pl
from jax.experimental.pallas import tpu as pltpu
from jax.sharding import Mesh, PartitionSpec as P


LEAF = ("xh", "z", "c")
GROUP = ("pole", "xh")
RING = ("z", "c")
XH, Z, C, POLES = 2, 8, 2, 8
LEAVES = XH * Z * C
SN = 256
HALF = SN // 2
RB = 8
BLOCKS = 32
SEL = 16
F32 = jnp.float32
BF16 = jnp.bfloat16


def leaf_perm(move):
    pairs = []
    for xh in range(XH):
        for z in range(Z):
            for c in range(C):
                a, b, d = move(xh, z, c)
                pairs.append(((xh * Z + z) * C + c, ((a % XH) * Z + b % Z) * C + d % C))
    return pairs


Z_UP = leaf_perm(lambda xh, z, c: (xh, z + 1, c))
Z_DOWN = leaf_perm(lambda xh, z, c: (xh, z - 1, c))
X_SWAP = leaf_perm(lambda xh, z, c: (xh + 1, z, c))
C_SWAP = leaf_perm(lambda xh, z, c: (xh, z, c + 1))


def send(value, perm):
    return lax.ppermute(value, LEAF, perm)


def vmem():
    return pl.BlockSpec(memory_space=pltpu.VMEM)


def room(mib):
    return pltpu.CompilerParams(vmem_limit_bytes=mib << 20)


def near(shape, kind=F32):
    return pltpu.VMEM(shape, kind)


def held(*values):
    return [pltpu.with_memory_space_constraint(value, pltpu.VMEM) for value in values]


def smem():
    return pl.BlockSpec(memory_space=pltpu.SMEM)


def pick_kernel(sel_ref, front_ref, out_ref, sems):
    copies = [
        pltpu.make_async_copy(
            front_ref.at[0, :, :, pl.ds(pl.multiple_of(sel_ref[r] * SN, SN), SN)], out_ref.at[r], sems.at[r]
        )
        for r in range(SEL)
    ]
    for copy in copies:
        copy.start()
    for copy in copies:
        copy.wait()


def pick_front(sel, front):
    return pl.pallas_call(
        pick_kernel,
        in_specs=[smem(), pl.BlockSpec(memory_space=pltpu.HBM)],
        out_specs=vmem(),
        out_shape=near((SEL, 2, SN, SN), BF16),
        scratch_shapes=[pltpu.SemaphoreType.DMA((SEL,))],
        compiler_params=room(2),
        name="pick_front",
    )(sel, pltpu.with_memory_space_constraint(front, pltpu.HBM))


def add_products(meta_ref, front_ref, acc_ref, pieces):
    for piece, places in pieces:
        for half, place in enumerate(places):

            @pl.when(meta_ref[place] == 1)
            def _(piece=piece, half=half, place=place):
                acc_ref[...] += jnp.dot(
                    front_ref[meta_ref[LEAVES + place]].reshape(2 * SN, SN),
                    piece[half * SN : (half + 1) * SN, :],
                    preferred_element_type=F32,
                )


def partial_product(meta, front, acc, pieces, places):
    given = 0 if acc is None else 1

    def kernel(meta_ref, front_ref, *refs):
        out_ref = refs[-1]
        out_ref[...] = refs[0][...] if given else jnp.zeros_like(out_ref)
        add_products(meta_ref, front_ref, out_ref, list(zip(refs[given:-1], places)))

    return pl.pallas_call(
        kernel,
        in_specs=[smem(), vmem()] + [vmem()] * (given + len(pieces)),
        out_specs=vmem(),
        out_shape=near((2 * SN, 2 * SN)),
        input_output_aliases={2: 0} if given else {},
        compiler_params=room(4),
        name="partial_product",
    )(meta, *held(front, *([acc] if given else []), *pieces))


def three_parts(value):
    first = value.astype(BF16)
    rest = value - first.astype(F32)
    second = rest.astype(BF16)
    return first, second, (rest - second.astype(F32)).astype(BF16)


def last_product(meta, weight, front, acc, panel, diag, pieces, places):
    def kernel(meta_ref, weight_ref, front_ref, acc_in, panel_ref, diag_ref, *refs):
        out_ref, acc_ref, den_ref, cor_ref = refs[-4:]
        acc_ref[...] = acc_in[...]
        add_products(meta_ref, front_ref, acc_ref, list(zip(refs[:-4], places)))
        keep = meta_ref[2 * LEAVES].astype(F32)
        lead = meta_ref[2 * LEAVES + 1].astype(F32)
        wr = weight_ref[0, 0]
        wi = weight_ref[0, 1]
        block_real = -(acc_ref[:SN, :SN] - acc_ref[SN:, SN:]) * keep
        block_imag = -(acc_ref[:SN, SN:] + acc_ref[SN:, :SN]) * keep
        density = wr * block_imag + wi * block_real
        other = wr * block_real - wi * block_imag
        den_ref[0] = density[:, :HALF]
        den_ref[1] = density[:, HALF:]
        schur = jnp.zeros((SN, SN), F32)
        for left, parts in ((panel_ref[:, :SN], three_parts(density)), (panel_ref[:, SN:], three_parts(other))):
            for part in parts:
                schur += lax.dot_general(left, part, (((0,), (0,)), ((), ())), preferred_element_type=F32)
        diag_real = diag_ref[0, :, :SN].astype(F32)
        diag_imag = diag_ref[0, :, SN:].astype(F32)
        cor_ref[...] = lead * (wr * diag_imag + wi * diag_real) - schur
        for q in range(POLES):
            for x in range(XH):
                g = q * XH + x
                out_ref[g, :BLOCKS] = den_ref[x, pl.ds(q, BLOCKS, stride=RB), :]
                out_ref[g, BLOCKS : BLOCKS + 16] = cor_ref[16 * g : 16 * g + 16, :HALF]
                out_ref[g, BLOCKS + 16 :] = cor_ref[16 * g : 16 * g + 16, HALF:]

    return pl.pallas_call(
        kernel,
        in_specs=[smem(), smem()] + [vmem()] * (4 + len(pieces)),
        out_specs=vmem(),
        out_shape=near((POLES * XH, 64, HALF)),
        scratch_shapes=[pltpu.VMEM((2 * SN, 2 * SN), F32), pltpu.VMEM((XH, SN, HALF), F32), pltpu.VMEM((SN, SN), F32)],
        compiler_params=room(8),
        name="last_product",
    )(meta, weight, *held(front, acc, panel), diag, *held(*pieces))


def route_kernel(place_ref, got_ref, out_ref, row_ref):
    corner = got_ref[0, BLOCKS:]
    for g in range(1, POLES * XH):
        corner += got_ref[g, BLOCKS:]
    for x in range(XH):
        rows = got_ref[x, :BLOCKS]
        for q in range(1, POLES):
            rows += got_ref[q * XH + x, :BLOCKS]
        row_ref[x * BLOCKS : (x + 1) * BLOCKS] = rows
    for h in range(Z * C):
        out_ref[h, :8] = jnp.zeros((8, HALF), F32)
        out_ref[h, 8:] = corner
    for b in range(XH * BLOCKS):
        place = place_ref[b]
        out_ref[place // 8, pl.ds(place % 8, 1), :] = row_ref[b : b + 1, :]


def route(place, got):
    return pl.pallas_call(
        route_kernel,
        in_specs=[smem(), vmem()],
        out_specs=vmem(),
        out_shape=near((Z * C, 40, HALF)),
        scratch_shapes=[pltpu.VMEM((XH * BLOCKS, HALF), F32)],
        compiler_params=room(4),
        name="route",
    )(place, *held(got))


def spread_kernel(got_ref, out_ref):
    corner = got_ref[0, 8:]
    for h in range(1, Z * C):
        corner += got_ref[h, 8:]
    for x in range(XH):
        for source in range(XH):
            for h in range(Z * C):
                row = 4 * x + 2 * source
                slot = (source * Z * C + h) * 2
                for q in range(POLES):
                    out_ref[q * XH + x, slot : slot + 2] = got_ref[h, row : row + 2]
    for g in range(POLES * XH):
        out_ref[g, 64:] = corner


def spread(got):
    return pl.pallas_call(
        spread_kernel,
        in_specs=[vmem()],
        out_specs=vmem(),
        out_shape=near((POLES * XH, 96, HALF)),
        compiler_params=room(4),
        name="spread",
    )(*held(got))


def finish_kernel(got_ref, owned_ref, diag_ref, row_ref):
    for q in range(POLES):
        for x in range(XH):
            g = q * XH + x
            row_ref[x, pl.ds(q, 64, stride=RB), :] = got_ref[g, :64]
            diag_ref[16 * g : 16 * g + 16, :HALF] = got_ref[g, 64:80]
            diag_ref[16 * g : 16 * g + 16, HALF:] = got_ref[g, 80:]
    for x in range(XH):
        owned_ref[:, x * HALF : (x + 1) * HALF] = row_ref[x]


def finish(got):
    return pl.pallas_call(
        finish_kernel,
        in_specs=[vmem()],
        out_specs=[vmem(), vmem()],
        out_shape=[jax.ShapeDtypeStruct((64 * RB, SN), F32), jax.ShapeDtypeStruct((SN, SN), F32)],
        scratch_shapes=[pltpu.VMEM((XH, 64 * RB, HALF), F32)],
        compiler_params=room(6),
        name="finish",
    )(*held(got))


def body(inverse_front, factor_panel, diag_inverse, pole_weight, structure, block_owner):
    xh, z, c = (lax.axis_index(name) for name in LEAF)
    own = factor_panel[0]

    dz = jnp.array([0, 0, -1, -1, 1, 1, -2, -2, 2, 2, -3, -3, 3, 3, 4, 4], jnp.int32)
    dx = jnp.array([0, 1] * 8, jnp.int32)
    chip = ((xh + dx) % XH) * Z + (z + dz) % Z
    origin = jnp.concatenate([chip * C + c, chip * C + (1 - c)])
    ids = jnp.arange(LEAVES, dtype=jnp.int32)
    kept = jnp.sum(jnp.where(origin[:, None] == ids[None, :], structure[None, :], 0), axis=1)
    place = jnp.sum(jnp.where(ids[None, :] < ids[:, None], kept[None, :], 0), axis=1)
    chosen = jnp.sum(
        jnp.where((place[None, :] == ids[:SEL, None]) & (kept[None, :] == 1), origin[None, :], 0), axis=1
    )
    lead = (origin[:1] == 0).astype(jnp.int32)
    meta = jnp.concatenate([kept, jnp.minimum(place, SEL - 1), kept[:1], lead])

    owners = block_owner[:, 0]
    same = (owners[:, None] == owners[None, :]) & (ids[None, :] < ids[:, None])
    slot = owners * 2 + jnp.sum(same.astype(jnp.int32), axis=1)
    slot_other = send(slot, X_SWAP)
    slots = jnp.concatenate([jnp.where(xh == 0, slot, slot_other), jnp.where(xh == 0, slot_other, slot)])
    source = jnp.arange(XH * BLOCKS, dtype=jnp.int32) // BLOCKS
    owner = slots // 2
    rows = (owner % (Z * C)) * 8 + (owner // (Z * C)) * 4 + source * 2 + slots % 2

    front = pick_front(chosen, inverse_front)

    pair = jnp.concatenate([own, send(own, X_SWAP)], axis=0)
    up, down = [pair], [pair]
    for _ in range(1, 4):
        up.append(send(up[-1], Z_UP))
        down.append(send(down[-1], Z_DOWN))
    up_last = send(up[3][:SN], Z_UP)
    down_last = send(down[3][SN:], Z_DOWN)
    pieces = [pair, up[1], down[1], up[2], down[2], up[3], down[3], up_last, down_last]
    places = [(0, 1), (2, 3), (4, 5), (6, 7), (8, 9), (10, 11), (12, 13), (14,), (15,)]
    for k in range(9):
        pieces.append(send(pieces[k], C_SWAP))
        places.append(tuple(p + 16 for p in places[k]))

    def some(numbers):
        return [pieces[k] for k in numbers], [places[k] for k in numbers]

    acc = partial_product(meta, front, None, *some((0, 1, 2, 9)))
    acc = partial_product(meta, front, acc, *some((10, 11, 3, 4)))
    acc = partial_product(meta, front, acc, *some((12, 13, 5, 6)))
    parts = last_product(meta, pole_weight, front, acc, own, diag_inverse, *some((14, 15, 7, 8, 16, 17)))
    parts = lax.all_to_all(parts, GROUP, 0, 0, tiled=True)
    parts = lax.all_to_all(route(rows, parts), RING, 0, 0, tiled=True)
    parts = lax.all_to_all(spread(parts), GROUP, 0, 0, tiled=True)
    owned, diag = finish(parts)
    return owned.reshape(64, RB, SN), diag


def solution(mesh):
    split = Mesh(mesh.devices.reshape(POLES, XH, Z, C), ("pole", "xh", "z", "c"))
    placed = (
        P("pole", None, LEAF, None),
        P("pole", LEAF, None),
        P("pole", None, None),
        P("pole", None),
        P(),
        P(LEAF, None),
    )
    return jax.shard_map(body, mesh=split, in_specs=placed, out_specs=(P(LEAF, None, None), P()), check_vma=False)
```

```python
import jax
import jax.numpy as jnp
from jax import lax
from jax.experimental import pallas as pl
from jax.experimental.pallas import tpu as pltpu
from jax.sharding import Mesh, PartitionSpec as P


LEAF = ("xh", "z", "c")
PLANE = ("pole", "xh", "c")
XH, Z, C, POLES = 2, 8, 2, 8
LEAVES = XH * Z * C
SN = 256
HALF = SN // 2
QUARTER = SN // 4
PLANES = 32
SOURCES = 4
RB = 8
BLOCKS = 32
SEL = 16
F32 = jnp.float32
BF16 = jnp.bfloat16


def leaf_perm(move):
    pairs = []
    for xh in range(XH):
        for z in range(Z):
            for c in range(C):
                a, b, d = move(xh, z, c)
                pairs.append(((xh * Z + z) * C + c, ((a % XH) * Z + b % Z) * C + d % C))
    return pairs


Z_FORTH = leaf_perm(lambda xh, z, c: (xh, z + 1 - 2 * c, c))
Z_BACK = leaf_perm(lambda xh, z, c: (xh, z - 1 + 2 * c, c))
X_SWAP = leaf_perm(lambda xh, z, c: (xh + 1, z, c))
DIAGONAL = leaf_perm(lambda xh, z, c: (xh + 1, z + 1 - 2 * c, c))
C_SWAP = leaf_perm(lambda xh, z, c: (xh, z, c + 1))


PANELS = (
    ("own", 0, 0),
    ("b1", 1, 0),
    ("x0", 0, 1),
    ("f1", -1, 0),
    ("f2", -2, 0),
    ("b2", 2, 0),
    ("y1", 1, 1),
    ("x1", -1, 1),
    ("f3", -3, 0),
    ("b3", 3, 0),
    ("y2", 2, 1),
    ("x2", -2, 1),
    ("f4", -4, 0),
    ("y3", 3, 1),
    ("x3", -3, 1),
    ("x4", -4, 1),
)


def send(value, perm):
    return lax.ppermute(value, LEAF, perm)


def vmem():
    return pl.BlockSpec(memory_space=pltpu.VMEM)


def room(mib):
    return pltpu.CompilerParams(vmem_limit_bytes=mib << 20)


def near(shape, kind=F32):
    return pltpu.VMEM(shape, kind)


def held(*values):
    return [pltpu.with_memory_space_constraint(value, pltpu.VMEM) for value in values]


def smem():
    return pl.BlockSpec(memory_space=pltpu.SMEM)


def lane_places(structure_ref, xh, z, lane):
    places, count = [], jnp.int32(0)
    for _, dz, dx in PANELS:
        leaf = (((xh + dx) & (XH - 1)) * Z + ((z + (1 - 2 * lane) * dz) & (Z - 1))) * C + lane
        kept = structure_ref[leaf]
        places.append((leaf, kept, count))
        count = count + kept
    return places


def pick_kernel(structure_ref, front_ref, keep_ref, give_ref, sems):
    xh, z, c = (lax.axis_index(name) for name in LEAF)
    copies = []
    for which, (lane, out_ref) in enumerate(((c, keep_ref), (1 - c, give_ref))):
        for leaf, kept, count in lane_places(structure_ref, xh, z, lane):
            copy = pltpu.make_async_copy(
                front_ref.at[0, :, :, pl.ds(pl.multiple_of(leaf * SN, SN), SN)],
                out_ref.at[count],
                sems.at[which, count],
            )
            copies.append((kept, copy))
    for kept, copy in copies:
        pl.when(kept == 1)(copy.start)
    for kept, copy in copies:
        pl.when(kept == 1)(copy.wait)


def pick_front(structure, front):
    return pl.pallas_call(
        pick_kernel,
        in_specs=[smem(), pl.BlockSpec(memory_space=pltpu.HBM)],
        out_specs=[vmem(), vmem()],
        out_shape=[near((SEL, 2, SN, SN), BF16)] * 2,
        scratch_shapes=[pltpu.SemaphoreType.DMA((2, SEL))],
        compiler_params=room(2),
        name="pick_front",
    )(structure, pltpu.with_memory_space_constraint(front, pltpu.HBM))


def add_products(structure_ref, keep_ref, got_ref, acc_ref, pieces):
    all_places = lane_places(structure_ref, *(lax.axis_index(name) for name in LEAF))
    for piece, places in pieces:
        for half, place in enumerate(places):

            _, kept, count = all_places[place]

            @pl.when(kept == 1)
            def _(piece=piece, half=half, count=count):
                panel = piece[half * SN : (half + 1) * SN, :]
                for k, front_ref in enumerate((keep_ref, got_ref)):
                    acc_ref[k] += jnp.dot(
                        front_ref[count].reshape(2 * SN, SN), panel, preferred_element_type=F32
                    )


def partial_product(structure, keep, got, acc, pieces, places):
    given = 0 if acc is None else 1

    def kernel(structure_ref, keep_ref, got_ref, *refs):
        out_ref = refs[-1]
        out_ref[...] = refs[0][...] if given else jnp.zeros_like(out_ref)
        add_products(structure_ref, keep_ref, got_ref, out_ref, list(zip(refs[given:-1], places)))

    return pl.pallas_call(
        kernel,
        in_specs=[smem()] + [vmem()] * (2 + given + len(pieces)),
        out_specs=vmem(),
        out_shape=near((2, 2 * SN, 2 * SN)),
        input_output_aliases={3: 0} if given else {},
        compiler_params=room(4),
        name="partial_product",
    )(structure, *held(keep, got, *([acc] if given else []), *pieces))


def low_lanes(shape):
    return lax.broadcasted_iota(jnp.int32, shape, 1) < QUARTER


def turned(value):
    return pltpu.roll(value, QUARTER, 1)


def pack(out_ref, g, low, first, second):
    count = first.shape[0]
    out_ref[g, :count] = jnp.where(low, first, turned(second))
    out_ref[g + 1, :count] = jnp.where(low, turned(first), second)


def last_product(structure, weight, keep, got, acc, pieces, places):
    def kernel(structure_ref, weight_ref, keep_ref, got_ref, acc_in, *refs):
        own_ref, other_ref, acc_ref = refs[-3:]
        acc_ref[...] = acc_in[...]
        add_products(structure_ref, keep_ref, got_ref, acc_ref, list(zip(refs[:-3], places)))
        wr = weight_ref[0, 0]
        wi = weight_ref[0, 1]
        for k, out_ref in enumerate((own_ref, other_ref)):
            block_real = acc_ref[k, SN:, SN:] - acc_ref[k, :SN, :SN]
            block_imag = -(acc_ref[k, :SN, SN:] + acc_ref[k, SN:, :SN])
            out_ref[0] = wr * block_imag + wi * block_real
            out_ref[1] = wr * block_real - wi * block_imag

    return pl.pallas_call(
        kernel,
        in_specs=[smem(), smem()] + [vmem()] * (3 + len(pieces)),
        out_specs=[vmem(), vmem()],
        out_shape=[near((2, SN, SN))] * 2,
        scratch_shapes=[pltpu.VMEM((2, 2 * SN, 2 * SN), F32)],
        compiler_params=room(8),
        name="last_product",
    )(structure, weight, *held(keep, got, acc, *pieces))


def three_parts(value):
    first = value.astype(BF16)
    rest = value - first.astype(F32)
    second = rest.astype(BF16)
    return first, second, (rest - second.astype(F32)).astype(BF16)


def weigh(structure, weight, own, other, panel, diag):
    def kernel(structure_ref, weight_ref, own_ref, other_ref, panel_ref, diag_ref, out_ref, den_ref, cor_ref):
        xh, z, c = (lax.axis_index(name) for name in LEAF)
        leaf = (xh * Z + z) * C + c
        row = structure_ref[leaf].astype(F32)
        lead = (leaf == 0).astype(F32)
        wr = weight_ref[0, 0]
        wi = weight_ref[0, 1]
        density = (own_ref[0] + other_ref[0]) * row
        other = (own_ref[1] + other_ref[1]) * row
        den_ref[0] = density[:, :HALF]
        den_ref[1] = density[:, HALF:]
        schur = jnp.zeros((SN, SN), F32)
        for left, parts in ((panel_ref[:, :SN], three_parts(density)), (panel_ref[:, SN:], three_parts(other))):
            for part in parts:
                schur += lax.dot_general(left, part, (((0,), (0,)), ((), ())), preferred_element_type=F32)
        diag_real = diag_ref[0, :, :SN].astype(F32)
        diag_imag = diag_ref[0, :, SN:].astype(F32)
        cor_ref[...] = lead * (wr * diag_imag + wi * diag_real) - schur
        low = low_lanes((BLOCKS // 2, HALF))
        for q in range(POLES):
            for x in range(XH):
                rows = den_ref[x, pl.ds(q, BLOCKS, stride=RB), :]
                pack(out_ref, (q * XH + x) * C, low, rows[: BLOCKS // 2], rows[BLOCKS // 2 :])
        for g in range(PLANES):
            out_ref[g, 16:24] = cor_ref[8 * g : 8 * g + 8, :HALF]
            out_ref[g, 24:] = cor_ref[8 * g : 8 * g + 8, HALF:]

    return pl.pallas_call(
        kernel,
        in_specs=[smem(), smem()] + [vmem()] * 4,
        out_specs=vmem(),
        out_shape=near((PLANES, 32, HALF)),
        scratch_shapes=[pltpu.VMEM((XH, SN, HALF), F32), pltpu.VMEM((SN, SN), F32)],
        compiler_params=room(6),
        name="weigh",
    )(structure, weight, *held(own, other, panel), diag)


def route_kernel(near_ref, far_ref, got_ref, out_ref, row_ref):
    corner = got_ref[0, 16:]
    for g in range(1, PLANES):
        corner += got_ref[g, 16:]
    for source in range(SOURCES):
        rows = got_ref[source, :16]
        for q in range(1, POLES):
            rows += got_ref[q * SOURCES + source, :16]
        other = turned(rows)
        row_ref[0, source * BLOCKS : source * BLOCKS + 16] = rows
        row_ref[0, source * BLOCKS + 16 : source * BLOCKS + 32] = other
        row_ref[1, source * BLOCKS : source * BLOCKS + 16] = other
        row_ref[1, source * BLOCKS + 16 : source * BLOCKS + 32] = rows
    for z in range(Z):
        out_ref[z, :16] = jnp.zeros((16, HALF), F32)
        out_ref[z, 16:] = corner
    xh, c = lax.axis_index("xh"), lax.axis_index("c")
    high = lax.broadcasted_iota(jnp.int32, (1, HALF), 1) // QUARTER
    for dx, places in enumerate((near_ref, far_ref)):
        for dc in range(C):
            source = (xh ^ dx) * C + (c ^ dc)
            for b in range(BLOCKS):
                place = places[dc, b]
                rank = place & 1
                row = pl.ds(((place >> 1) & 15) + source, 1)
                taken = row_ref[rank, pl.ds(source * BLOCKS + b, 1), :]
                z = place >> 5
                out_ref[z, row, :] = jnp.where(high == rank, taken, out_ref[z, row, :])


def route(here, there, got):
    return pl.pallas_call(
        route_kernel,
        in_specs=[smem(), smem(), vmem()],
        out_specs=vmem(),
        out_shape=near((Z, 32, HALF)),
        scratch_shapes=[pltpu.VMEM((2, SOURCES * BLOCKS, HALF), F32)],
        compiler_params=room(4),
        name="route",
    )(here, there, *held(got))


def spread_kernel(structure_ref, got_ref, out_ref, row_ref):
    corner = got_ref[0, 16:]
    for z in range(1, Z):
        corner += got_ref[z, 16:]
    count = jnp.int32(0)
    for leaf in range(LEAVES):

        @pl.when(structure_ref[leaf] == 1)
        def _(leaf=leaf, count=count):
            source = (leaf // (Z * C)) * C + leaf % C
            for owner in range(SOURCES):
                row = owner * SOURCES + source
                row_ref[owner, pl.ds(count, 1), :] = got_ref[(leaf // C) % Z, row : row + 1, :]

        count = count + structure_ref[leaf]
    for owner in range(SOURCES):
        rows = row_ref[owner]
        for q in range(POLES):
            out_ref[q * SOURCES + owner, :SEL] = rows
    for g in range(PLANES):
        out_ref[g, SEL:] = corner


def spread(structure, got):
    return pl.pallas_call(
        spread_kernel,
        in_specs=[smem(), vmem()],
        out_specs=vmem(),
        out_shape=near((PLANES, SEL + 16, HALF)),
        scratch_shapes=[pltpu.VMEM((SOURCES, SEL, HALF), F32)],
        compiler_params=room(4),
        name="spread",
    )(structure, *held(got))


def finish_kernel(structure_ref, got_ref, owned_ref, diag_ref, row_ref):
    low = low_lanes((SEL, HALF))
    for q in range(POLES):
        for x in range(XH):
            g = (q * XH + x) * C
            first, second = got_ref[g, :SEL], got_ref[g + 1, :SEL]
            row_ref[x, pl.ds(q, SEL, stride=2 * RB), :] = jnp.where(low, first, turned(second))
            row_ref[x, pl.ds(q + RB, SEL, stride=2 * RB), :] = jnp.where(low, turned(first), second)
    for g in range(PLANES):
        diag_ref[8 * g : 8 * g + 8, :HALF] = got_ref[g, SEL : SEL + 8]
        diag_ref[8 * g : 8 * g + 8, HALF:] = got_ref[g, SEL + 8 :]
    count = jnp.int32(0)
    for leaf in range(LEAVES):
        place = slice(leaf * 2 * RB, (leaf + 1) * 2 * RB)

        @pl.when(structure_ref[leaf] == 1)
        def _(place=place, count=count):
            for x in range(XH):
                owned_ref[place, x * HALF : (x + 1) * HALF] = row_ref[
                    x, pl.ds(pl.multiple_of(count * 2 * RB, 2 * RB), 2 * RB), :
                ]

        @pl.when(structure_ref[leaf] != 1)
        def _(place=place):
            owned_ref[place] = jnp.zeros((2 * RB, SN), F32)

        count = count + structure_ref[leaf]


def finish(structure, got):
    return pl.pallas_call(
        finish_kernel,
        in_specs=[smem(), vmem()],
        out_specs=[vmem(), vmem()],
        out_shape=[jax.ShapeDtypeStruct((64 * RB, SN), F32), jax.ShapeDtypeStruct((SN, SN), F32)],
        scratch_shapes=[pltpu.VMEM((XH, SEL * 2 * RB, HALF), F32)],
        compiler_params=room(6),
        name="finish",
    )(structure, *held(got))


def body(inverse_front, factor_panel, diag_inverse, pole_weight, structure, block_owner):
    xh, z, c = (lax.axis_index(name) for name in LEAF)
    own = factor_panel[0]

    ids = jnp.arange(LEAVES, dtype=jnp.int32)
    owners = block_owner[:, 0]
    same = (owners[:, None] == owners[None, :]) & (ids[None, :] < ids[:, None])
    rank = jnp.sum(same.astype(jnp.int32), axis=1)
    member = (owners // (Z * C)) * C + owners % C
    place = (((owners // C) % Z) * 16 + member * SOURCES) * 2 + rank
    here = jnp.stack([place, send(place, C_SWAP)])
    there = send(here, X_SWAP)

    keep, give = pick_front(structure, inverse_front)
    got = send(give, C_SWAP)

    f1 = send(own, Z_FORTH)
    b1 = send(own, Z_BACK)
    x0 = send(own, X_SWAP)
    f2 = send(f1, Z_FORTH)
    b2 = send(b1, Z_BACK)
    y1 = send(x0, Z_BACK)
    x1 = send(f1, X_SWAP)
    f3 = send(f2, Z_FORTH)
    b3 = send(b2, Z_BACK)
    y2 = send(y1, Z_BACK)
    x2 = send(f2, X_SWAP)
    f4 = send(f3, Z_FORTH)
    y3 = send(y2, Z_BACK)
    x3 = send(f3, X_SWAP)
    x4 = send(f3, DIAGONAL)

    acc = partial_product(structure, keep, got, None, [own, b1, x0, f1], [(0,), (1,), (2,), (3,)])
    acc = partial_product(structure, keep, got, acc, [f2, b2, y1, x1], [(4,), (5,), (6,), (7,)])
    acc = partial_product(structure, keep, got, acc, [f3, b3, y2, x2], [(8,), (9,), (10,), (11,)])
    late, there = lax.optimization_barrier((structure, there))
    mine, theirs = last_product(
        late, pole_weight, keep, got, acc, [f4, y3, x3, x4], [(12,), (13,), (14,), (15,)]
    )
    theirs = send(theirs, C_SWAP)
    parts = weigh(structure, pole_weight, mine, theirs, own, diag_inverse)
    parts = lax.all_to_all(parts, PLANE, 0, 0, tiled=True)
    parts = lax.all_to_all(route(here, there, parts), "z", 0, 0, tiled=True)
    parts = lax.all_to_all(spread(structure, parts), PLANE, 0, 0, tiled=True)
    owned, diag = finish(structure, parts)
    return owned.reshape(64, RB, SN), diag


def solution(mesh):
    split = Mesh(mesh.devices.reshape(POLES, XH, Z, C), ("pole", "xh", "z", "c"))
    placed = (
        P("pole", None, LEAF, None),
        P("pole", LEAF, None),
        P("pole", None, None),
        P("pole", None),
        P(),
        P(LEAF, None),
    )
    return jax.shard_map(
        body, mesh=split, in_specs=placed, out_specs=(P(LEAF, None, None), P()), check_vma=False
    )
```

```python
import jax
import jax.numpy as jnp
from jax import lax
from jax.experimental import pallas as pl
from jax.experimental.pallas import tpu as pltpu
from jax.sharding import Mesh, PartitionSpec as P


LEAF = ("xh", "z", "c")
PLANE = ("pole", "xh", "c")
XH, Z, C, POLES = 2, 8, 2, 8
LEAVES = XH * Z * C
SN = 256
HALF = SN // 2
QUARTER = SN // 4
PLANES = 32
SOURCES = 4
RB = 8
BLOCKS = 32
SEL = 16
F32 = jnp.float32
BF16 = jnp.bfloat16


def leaf_perm(move):
    pairs = []
    for xh in range(XH):
        for z in range(Z):
            for c in range(C):
                a, b, d = move(xh, z, c)
                pairs.append(((xh * Z + z) * C + c, ((a % XH) * Z + b % Z) * C + d % C))
    return pairs


Z_FORTH = leaf_perm(lambda xh, z, c: (xh, z + 1 - 2 * c, c))
Z_BACK = leaf_perm(lambda xh, z, c: (xh, z - 1 + 2 * c, c))
X_SWAP = leaf_perm(lambda xh, z, c: (xh + 1, z, c))
DIAGONAL = leaf_perm(lambda xh, z, c: (xh + 1, z + 1 - 2 * c, c))
C_SWAP = leaf_perm(lambda xh, z, c: (xh, z, c + 1))


PANELS = (
    ("own", 0, 0),
    ("b1", 1, 0),
    ("x0", 0, 1),
    ("f1", -1, 0),
    ("f2", -2, 0),
    ("b2", 2, 0),
    ("y1", 1, 1),
    ("x1", -1, 1),
    ("f3", -3, 0),
    ("b3", 3, 0),
    ("y2", 2, 1),
    ("x2", -2, 1),
    ("f4", -4, 0),
    ("y3", 3, 1),
    ("x3", -3, 1),
    ("x4", -4, 1),
)


def send(value, perm):
    return lax.ppermute(value, LEAF, perm)


def vmem():
    return pl.BlockSpec(memory_space=pltpu.VMEM)


def room(mib):
    return pltpu.CompilerParams(vmem_limit_bytes=mib << 20)


def near(shape, kind=F32):
    return pltpu.VMEM(shape, kind)


def held(*values):
    return [pltpu.with_memory_space_constraint(value, pltpu.VMEM) for value in values]


def smem():
    return pl.BlockSpec(memory_space=pltpu.SMEM)


def lane_places(structure_ref, xh, z, lane):
    places, count = [], jnp.int32(0)
    for _, dz, dx in PANELS:
        leaf = (((xh + dx) & (XH - 1)) * Z + ((z + (1 - 2 * lane) * dz) & (Z - 1))) * C + lane
        kept = structure_ref[leaf]
        places.append((leaf, kept, count))
        count = count + kept
    return places


def pick_kernel(structure_ref, front_ref, keep_ref, give_ref, sems):
    xh, z, c = (lax.axis_index(name) for name in LEAF)
    copies = []
    for which, (lane, out_ref) in enumerate(((c, keep_ref), (1 - c, give_ref))):
        for leaf, kept, count in lane_places(structure_ref, xh, z, lane):
            copy = pltpu.make_async_copy(
                front_ref.at[0, :, :, pl.ds(pl.multiple_of(leaf * SN, SN), SN)],
                out_ref.at[count],
                sems.at[which, count],
            )
            copies.append((kept, copy))
    for kept, copy in copies:
        pl.when(kept == 1)(copy.start)
    for kept, copy in copies:
        pl.when(kept == 1)(copy.wait)


def pick_front(structure, front):
    return pl.pallas_call(
        pick_kernel,
        in_specs=[smem(), pl.BlockSpec(memory_space=pltpu.HBM)],
        out_specs=[vmem(), vmem()],
        out_shape=[near((SEL, 2, SN, SN), BF16)] * 2,
        scratch_shapes=[pltpu.SemaphoreType.DMA((2, SEL))],
        compiler_params=room(2),
        name="pick_front",
    )(structure, pltpu.with_memory_space_constraint(front, pltpu.HBM))


def add_products(structure_ref, keep_ref, got_ref, acc_ref, pieces):
    all_places = lane_places(structure_ref, *(lax.axis_index(name) for name in LEAF))
    for piece, places in pieces:
        for half, place in enumerate(places):

            _, kept, count = all_places[place]

            @pl.when(kept == 1)
            def _(piece=piece, half=half, count=count):
                panel = piece[half * SN : (half + 1) * SN, :]
                for k, front_ref in enumerate((keep_ref, got_ref)):
                    acc_ref[k] += jnp.dot(
                        front_ref[count].reshape(2 * SN, SN), panel, preferred_element_type=F32
                    )


def partial_product(structure, keep, got, acc, pieces, places):
    given = 0 if acc is None else 1

    def kernel(structure_ref, keep_ref, got_ref, *refs):
        out_ref = refs[-1]
        out_ref[...] = refs[0][...] if given else jnp.zeros_like(out_ref)
        add_products(structure_ref, keep_ref, got_ref, out_ref, list(zip(refs[given:-1], places)))

    return pl.pallas_call(
        kernel,
        in_specs=[smem()] + [vmem()] * (2 + given + len(pieces)),
        out_specs=vmem(),
        out_shape=near((2, 2 * SN, 2 * SN)),
        input_output_aliases={3: 0} if given else {},
        compiler_params=room(4),
        name="partial_product",
    )(structure, *held(keep, got, *([acc] if given else []), *pieces))


def low_lanes(shape):
    return lax.broadcasted_iota(jnp.int32, shape, 1) < QUARTER


def turned(value):
    return pltpu.roll(value, QUARTER, 1)


def pack(out_ref, g, low, first, second):
    count = first.shape[0]
    out_ref[g, :count] = jnp.where(low, first, turned(second))
    out_ref[g + 1, :count] = jnp.where(low, turned(first), second)


def last_product(structure, weight, keep, got, acc, pieces, places):
    def kernel(structure_ref, weight_ref, keep_ref, got_ref, acc_in, *refs):
        own_ref, other_ref, acc_ref = refs[-3:]
        acc_ref[...] = acc_in[...]
        add_products(structure_ref, keep_ref, got_ref, acc_ref, list(zip(refs[:-3], places)))
        wr = weight_ref[0, 0]
        wi = weight_ref[0, 1]
        for k, out_ref in enumerate((own_ref, other_ref)):
            block_real = acc_ref[k, SN:, SN:] - acc_ref[k, :SN, :SN]
            block_imag = -(acc_ref[k, :SN, SN:] + acc_ref[k, SN:, :SN])
            out_ref[0] = wr * block_imag + wi * block_real
            out_ref[1] = wr * block_real - wi * block_imag

    return pl.pallas_call(
        kernel,
        in_specs=[smem(), smem()] + [vmem()] * (3 + len(pieces)),
        out_specs=[vmem(), vmem()],
        out_shape=[near((2, SN, SN))] * 2,
        scratch_shapes=[pltpu.VMEM((2, 2 * SN, 2 * SN), F32)],
        compiler_params=room(8),
        name="last_product",
    )(structure, weight, *held(keep, got, acc, *pieces))


def three_parts(value):
    first = value.astype(BF16)
    rest = value - first.astype(F32)
    second = rest.astype(BF16)
    return first, second, (rest - second.astype(F32)).astype(BF16)


def weigh(structure, weight, own, other, panel, diag):
    def kernel(structure_ref, weight_ref, own_ref, other_ref, panel_ref, diag_ref, out_ref, den_ref, cor_ref):
        xh, z, c = (lax.axis_index(name) for name in LEAF)
        leaf = (xh * Z + z) * C + c
        row = structure_ref[leaf].astype(F32)
        lead = (leaf == 0).astype(F32)
        wr = weight_ref[0, 0]
        wi = weight_ref[0, 1]
        density = (own_ref[0] + other_ref[0]) * row
        other = (own_ref[1] + other_ref[1]) * row
        den_ref[0] = density[:, :HALF]
        den_ref[1] = density[:, HALF:]
        schur = jnp.zeros((SN, SN), F32)
        for left, parts in ((panel_ref[:, :SN], three_parts(density)), (panel_ref[:, SN:], three_parts(other))):
            for part in parts:
                schur += lax.dot_general(left, part, (((0,), (0,)), ((), ())), preferred_element_type=F32)
        diag_real = diag_ref[0, :, :SN].astype(F32)
        diag_imag = diag_ref[0, :, SN:].astype(F32)
        cor_ref[...] = lead * (wr * diag_imag + wi * diag_real) - schur
        low = low_lanes((BLOCKS // 2, HALF))
        for q in range(POLES):
            for x in range(XH):
                rows = den_ref[x, pl.ds(q, BLOCKS, stride=RB), :]
                pack(out_ref, (q * XH + x) * C, low, rows[: BLOCKS // 2], rows[BLOCKS // 2 :])
        for g in range(PLANES):
            out_ref[g, 16:24] = cor_ref[8 * g : 8 * g + 8, :HALF]
            out_ref[g, 24:] = cor_ref[8 * g : 8 * g + 8, HALF:]

    return pl.pallas_call(
        kernel,
        in_specs=[smem(), smem()] + [vmem()] * 4,
        out_specs=vmem(),
        out_shape=near((PLANES, 32, HALF)),
        scratch_shapes=[pltpu.VMEM((XH, SN, HALF), F32), pltpu.VMEM((SN, SN), F32)],
        compiler_params=room(6),
        name="weigh",
    )(structure, weight, *held(own, other, panel), diag)


def route_kernel(near_ref, far_ref, got_ref, out_ref, row_ref):
    corner = got_ref[0, 16:]
    for g in range(1, PLANES):
        corner += got_ref[g, 16:]
    for source in range(SOURCES):
        rows = got_ref[source, :16]
        for q in range(1, POLES):
            rows += got_ref[q * SOURCES + source, :16]
        other = turned(rows)
        row_ref[0, source * BLOCKS : source * BLOCKS + 16] = rows
        row_ref[0, source * BLOCKS + 16 : source * BLOCKS + 32] = other
        row_ref[1, source * BLOCKS : source * BLOCKS + 16] = other
        row_ref[1, source * BLOCKS + 16 : source * BLOCKS + 32] = rows
    for z in range(Z):
        out_ref[z, :16] = jnp.zeros((16, HALF), F32)
        out_ref[z, 16:] = corner
    xh, c = lax.axis_index("xh"), lax.axis_index("c")
    high = lax.broadcasted_iota(jnp.int32, (1, HALF), 1) // QUARTER
    for dx, places in enumerate((near_ref, far_ref)):
        for dc in range(C):
            source = (xh ^ dx) * C + (c ^ dc)
            for b in range(BLOCKS):
                place = places[dc, b]
                rank = place & 1
                row = pl.ds(((place >> 1) & 15) + source, 1)
                taken = row_ref[rank, pl.ds(source * BLOCKS + b, 1), :]
                z = place >> 5
                out_ref[z, row, :] = jnp.where(high == rank, taken, out_ref[z, row, :])


def route(here, there, got):
    return pl.pallas_call(
        route_kernel,
        in_specs=[smem(), smem(), vmem()],
        out_specs=vmem(),
        out_shape=near((Z, 32, HALF)),
        scratch_shapes=[pltpu.VMEM((2, SOURCES * BLOCKS, HALF), F32)],
        compiler_params=room(4),
        name="route",
    )(here, there, *held(got))


def spread_kernel(structure_ref, got_ref, out_ref, row_ref):
    corner = got_ref[0, 16:]
    for z in range(1, Z):
        corner += got_ref[z, 16:]
    count = jnp.int32(0)
    for leaf in range(LEAVES):

        @pl.when(structure_ref[leaf] == 1)
        def _(leaf=leaf, count=count):
            source = (leaf // (Z * C)) * C + leaf % C
            for owner in range(SOURCES):
                row = owner * SOURCES + source
                row_ref[owner, pl.ds(count, 1), :] = got_ref[(leaf // C) % Z, row : row + 1, :]

        count = count + structure_ref[leaf]
    for owner in range(SOURCES):
        rows = row_ref[owner]
        for q in range(POLES):
            out_ref[q * SOURCES + owner, :SEL] = rows
    for g in range(PLANES):
        out_ref[g, SEL:] = corner


def spread(structure, got):
    return pl.pallas_call(
        spread_kernel,
        in_specs=[smem(), vmem()],
        out_specs=vmem(),
        out_shape=near((PLANES, SEL + 16, HALF)),
        scratch_shapes=[pltpu.VMEM((SOURCES, SEL, HALF), F32)],
        compiler_params=room(4),
        name="spread",
    )(structure, *held(got))


def finish_kernel(structure_ref, got_ref, owned_ref, diag_ref, row_ref):
    low = low_lanes((SEL, HALF))
    for q in range(POLES):
        for x in range(XH):
            g = (q * XH + x) * C
            first, second = got_ref[g, :SEL], got_ref[g + 1, :SEL]
            row_ref[x, pl.ds(q, SEL, stride=2 * RB), :] = jnp.where(low, first, turned(second))
            row_ref[x, pl.ds(q + RB, SEL, stride=2 * RB), :] = jnp.where(low, turned(first), second)
    for g in range(PLANES):
        diag_ref[8 * g : 8 * g + 8, :HALF] = got_ref[g, SEL : SEL + 8]
        diag_ref[8 * g : 8 * g + 8, HALF:] = got_ref[g, SEL + 8 :]
    count = jnp.int32(0)
    for leaf in range(LEAVES):
        place = slice(leaf * 2 * RB, (leaf + 1) * 2 * RB)

        kept = structure_ref[leaf]
        start = pl.multiple_of(jnp.minimum(count, SEL - 1) * 2 * RB, 2 * RB)
        for x in range(XH):
            rows = row_ref[x, pl.ds(start, 2 * RB), :]
            owned_ref[place, x * HALF : (x + 1) * HALF] = jnp.where(kept == 1, rows, 0.0)
        count = count + kept


def finish(structure, got):
    return pl.pallas_call(
        finish_kernel,
        in_specs=[smem(), vmem()],
        out_specs=[vmem(), vmem()],
        out_shape=[jax.ShapeDtypeStruct((64 * RB, SN), F32), jax.ShapeDtypeStruct((SN, SN), F32)],
        scratch_shapes=[pltpu.VMEM((XH, SEL * 2 * RB, HALF), F32)],
        compiler_params=room(6),
        name="finish",
    )(structure, *held(got))


def body(inverse_front, factor_panel, diag_inverse, pole_weight, structure, block_owner):
    xh, z, c = (lax.axis_index(name) for name in LEAF)
    own = factor_panel[0]

    ids = jnp.arange(LEAVES, dtype=jnp.int32)
    owners = block_owner[:, 0]
    same = (owners[:, None] == owners[None, :]) & (ids[None, :] < ids[:, None])
    rank = jnp.sum(same.astype(jnp.int32), axis=1)
    member = (owners // (Z * C)) * C + owners % C
    place = (((owners // C) % Z) * 16 + member * SOURCES) * 2 + rank
    here = jnp.stack([place, send(place, C_SWAP)])
    there = send(here, X_SWAP)

    keep, give = pick_front(structure, inverse_front)
    got = send(give, C_SWAP)

    f1 = send(own, Z_FORTH)
    b1 = send(own, Z_BACK)
    x0 = send(own, X_SWAP)
    f2 = send(f1, Z_FORTH)
    b2 = send(b1, Z_BACK)
    y1 = send(x0, Z_BACK)
    x1 = send(f1, X_SWAP)
    f3 = send(f2, Z_FORTH)
    b3 = send(b2, Z_BACK)
    y2 = send(y1, Z_BACK)
    x2 = send(f2, X_SWAP)
    f4 = send(f3, Z_FORTH)
    y3 = send(y2, Z_BACK)
    x3 = send(f3, X_SWAP)
    x4 = send(f3, DIAGONAL)

    acc = partial_product(structure, keep, got, None, [own, b1, x0, f1], [(0,), (1,), (2,), (3,)])
    acc = partial_product(structure, keep, got, acc, [f2, b2, y1, x1], [(4,), (5,), (6,), (7,)])
    acc = partial_product(structure, keep, got, acc, [f3, b3, y2, x2], [(8,), (9,), (10,), (11,)])
    late, there = lax.optimization_barrier((structure, there))
    mine, theirs = last_product(
        late, pole_weight, keep, got, acc, [f4, y3, x3, x4], [(12,), (13,), (14,), (15,)]
    )
    theirs = send(theirs, C_SWAP)
    parts = weigh(structure, pole_weight, mine, theirs, own, diag_inverse)
    parts = lax.all_to_all(parts, PLANE, 0, 0, tiled=True)
    parts = lax.all_to_all(route(here, there, parts), "z", 0, 0, tiled=True)
    parts = lax.all_to_all(spread(structure, parts), PLANE, 0, 0, tiled=True)
    owned, diag = finish(structure, parts)
    return owned.reshape(64, RB, SN), diag


def solution(mesh):
    split = Mesh(mesh.devices.reshape(POLES, XH, Z, C), ("pole", "xh", "z", "c"))
    placed = (
        P("pole", None, LEAF, None),
        P("pole", LEAF, None),
        P("pole", None, None),
        P("pole", None),
        P(),
        P(LEAF, None),
    )
    return jax.shard_map(
        body, mesh=split, in_specs=placed, out_specs=(P(LEAF, None, None), P()), check_vma=False
    )
```
